32 devices in a mesh: groups: 2 (over x), seq: 16 (over z, y, core).
Axes of the slice: x: 2, y: 2, z: 4, core: 2. Of those that a mesh axis runs over, the one named last changes fastest.
Arguments:
- hidden: bfloat16 [64, 16384], P('groups', 'seq'), parts along dimension 0, may hold values from -6 to 6
- w_query: bfloat16 [16384, 8192], P('seq'), may hold values from -0.046875 to 0.046875
- w_key: bfloat16 [16384, 512], P('seq'), may hold values from -0.25 to 0.25
- w_value: bfloat16 [16384, 512], P('seq'), may hold values from -0.1875 to 0.1875
- w_out: bfloat16 [8192, 16384], P(None, 'seq'), may hold values from -0.0625 to 0.0625
- prefix_keys: bfloat16 [65536, 512], P(('groups', 'seq')), parts along dimension 0, may hold values from -6 to 6
- prefix_values: bfloat16 [65536, 512], P(('groups', 'seq')), parts along dimension 0, may hold values from -6 to 6
- key_scales: float32 [512, 4], P(('groups', 'seq')), parts along dimension 0, may hold values from 1 to 2.5
- value_scales: float32 [512, 4], P(('groups', 'seq')), parts along dimension 0, may hold values from 0.5 to 2
- demo_keys: bfloat16 [32, 2048, 512], P('groups', 'seq'), parts along dimension 0, may hold values from -200 to 200
- demo_values: bfloat16 [32, 2048, 512], P('groups', 'seq'), parts along dimension 0, may hold values from -12 to 12
- task_ids: int32 [64], P('groups'), parts along dimension 0, may hold values from 0 to 15
- demo_lengths: int32 [32], P('groups'), parts along dimension 0, may hold values from 1 to 2048, 16384 in all
- offsets: int32 [64], P('groups'), parts along dimension 0, may hold values from 0 to 31
Outputs:
- mixed: bfloat16 [64, 16384], P('groups', 'seq'), parts along dimension 0
The draws below stay inside these ranges and needn't reach their ends.
There are 2 independent parts, one for each index of `groups`. The reference program is written for one: setup_inputs(seed, part) draws one part's arguments, and reference() takes and returns one part's arrays. A program takes and returns all parts, laid end to end along the dimension named above; an argument that names none is the same for every part. Nothing has to cross between parts.
Inputs may be any that keep to these rules, and one draw needn't show every extreme that they name: `demo_lengths`: the largest is exactly 2048.
All inputs are finite; a program needn't handle non-finite values.
Results may differ from the reference program's by a relative error of at most 0.007.
The reference program's roundings to bfloat16 on the way count: a program that leaves them out, or rounds other values in their place, can miss the bound.
Values may be sent and summed in bfloat16 or wider, within the bound.
A program may use at most 128 MiB of HBM per device.

```python
import math
import jax
import jax.numpy as jnp
import numpy as np
from jax import lax

D = 16384
HEADS = 64
KVH = 4
HD = 128
TASKS = 16
DEMO = 2048
BLK = 128
QTOK = 32
PREFIX = 32768


def draw_demo_keys(key, part):
    shape = (TASKS, DEMO, KVH * HD)
    return jnp.clip(3.5 * jax.random.normal(key, shape, jnp.float32), -21.0, 21.0).astype(jnp.bfloat16)


def with_ends(entries, key, least, top_value):
    index_at = [jax.random.randint(jax.random.fold_in(key, axis), (), 0, length) for axis, length in enumerate(entries.shape)]
    main_axis = entries.shape.index(max(entries.shape))
    beside = index_at[:main_axis] + [(index_at[main_axis] + 1) % entries.shape[main_axis]] + index_at[main_axis + 1:]
    return entries.at[tuple(index_at)].set(least).at[tuple(beside)].set(top_value)


def block_scale(stream_key, extent, shards, low, top_value):
    gain = 1.0
    for dim, shards_of in shards:
        heights = jax.random.uniform(jax.random.fold_in(jax.random.fold_in(stream_key, 6), dim), (shards_of,), jnp.float32, low / len(shards), top_value / len(shards))
        gain = gain * jnp.repeat(jnp.exp(heights), extent[dim] // shards_of).reshape((-1,) + (1,) * (len(extent) - 1 - dim))
    return gain


def profile(count, total, limit, slope):
    loads = [(1 << 20) // math.isqrt(grade ** slope) + 1 for grade in range(2, count + 1)]
    rest, counts = total - limit - (count - 1), [1] * (count - 1)
    while rest > 0:
        movable = [i for i in range(count - 1) if counts[i] < limit]
        mass, left = sum([loads[i] for i in movable]), rest
        for i in movable:
            extra = min(limit - counts[i], max(1, left * loads[i] // mass), rest)
            counts[i] = counts[i] + extra
            rest = rest - extra
    return np.array([limit] + counts)


def ragged_sizes(stream_key, number_of, total, bound, lean):
    if number_of == 2:
        one = jax.random.randint(stream_key, (), max(1, total - bound), min(bound, total - 1) + 1)
        return jnp.stack([one, total - one])
    tallies = jnp.asarray(profile(number_of, total, bound, lean), jnp.int32)
    couples = (number_of - 1) // 2
    source_of, receiver = tallies[1:1 + 2 * couples:2], tallies[2:2 + 2 * couples:2]
    margin = jnp.minimum(source_of - 1, bound - receiver)
    moved = jax.random.randint(jax.random.fold_in(stream_key, 1), (couples,), 0, 1 << 20) % (margin + 1)
    tallies = tallies.at[1:1 + 2 * couples:2].set(source_of - moved).at[2:2 + 2 * couples:2].set(receiver + moved)
    return tallies[jax.random.permutation(jax.random.fold_in(stream_key, 2), number_of)]


def centred(stream_key, dims, spread, limit, split=(), held_as=jnp.bfloat16):
    loudness = block_scale(stream_key, dims, split, -0.22, 0.18) if split else 1.0
    result = jax.random.normal(stream_key, dims, jnp.float32) * spread * loudness
    return jnp.minimum(jnp.maximum(result, -limit), limit).astype(held_as)


def setup_inputs(seed: int = 0, part: int = 0) -> dict:
    keys = jax.random.split(jax.random.key(seed), 15)
    part_keys = jax.random.split(jax.random.fold_in(keys[14], part), 15)
    hidden = centred(part_keys[0], (QTOK, D), 1.0, 6.0, ((1, 16),))
    w_query = centred(keys[1], (D, HEADS * HD), D ** -0.5, 0.046875, ((0, 16),))
    w_key = centred(keys[2], (D, KVH * HD), (D // 25) ** -0.5, 0.25, ((0, 16),))
    w_value = centred(keys[3], (D, KVH * HD), (D // 16) ** -0.5, 0.1875, ((0, 16),))
    w_out = centred(keys[4], (HEADS * HD, D), (HEADS * HD) ** -0.5, 0.0625, ((1, 16),))
    prefix_keys = centred(part_keys[5], (PREFIX, KVH * HD), 1.0, 6.0, ((0, 16),))
    prefix_values = centred(part_keys[6], (PREFIX, KVH * HD), 1.0, 6.0, ((0, 16),))
    key_scales = jnp.clip(jnp.exp(math.log(2.5) - 0.916290732 * jax.random.uniform(part_keys[7], (PREFIX // BLK, KVH), jnp.float32) ** block_scale(part_keys[7], (PREFIX // BLK, KVH), ((0, 16),), -0.2, 0.2)), 1.0, 2.5)
    value_scales = jnp.clip(jnp.exp(math.log(2.0) - 1.3862944 * jax.random.uniform(part_keys[8], (PREFIX // BLK, KVH), jnp.float32) ** block_scale(part_keys[8], (PREFIX // BLK, KVH), ((0, 16),), -0.2, 0.2)), 0.5, 2.0)
    demo_keys = draw_demo_keys(jax.random.fold_in(jax.random.fold_in(keys[14], part), 71), part)
    demo_values = centred(part_keys[10], (TASKS, DEMO, KVH * HD), 2.0, 12.0, ((1, 16),))
    task_ids = with_ends(jax.random.randint(part_keys[11], (QTOK,), 0, TASKS), jax.random.fold_in(part_keys[11], 1), 0, TASKS - 1).astype(jnp.int32)
    demo_lengths = ragged_sizes(part_keys[12], TASKS, TASKS * DEMO // 2, DEMO, 2).astype(jnp.int32)
    offsets = with_ends(jax.random.randint(part_keys[13], (QTOK,), 0, 32), jax.random.fold_in(part_keys[13], 1), 0, 31).astype(jnp.int32)
    return {"hidden": hidden, "w_query": w_query, "w_key": w_key, "w_value": w_value, "w_out": w_out, "prefix_keys": prefix_keys, "prefix_values": prefix_values, "key_scales": key_scales, "value_scales": value_scales, "demo_keys": demo_keys, "demo_values": demo_values, "task_ids": task_ids, "demo_lengths": demo_lengths, "offsets": offsets}


NEG = -1e+30

def one_head(args):
    q_rows, p_keys, p_vals, k_scale, v_scale, d_keys, d_vals, s_keys, s_vals, d_mask, s_mask = args
    inv = 1.0 / math.sqrt(HD)
    s_pre = jnp.dot(q_rows, p_keys.T, preferred_element_type=jnp.float32) * (k_scale[None, :] * inv)
    s_demo = jnp.where(d_mask, jnp.dot(q_rows, d_keys.T, preferred_element_type=jnp.float32) * inv, NEG)
    s_self = jnp.where(s_mask, jnp.dot(q_rows, s_keys.T, preferred_element_type=jnp.float32) * inv, NEG)
    top = jnp.maximum(jnp.maximum(lax.optimization_barrier(jnp.max(s_pre, axis=1)), lax.optimization_barrier(jnp.max(s_demo, axis=1))), lax.optimization_barrier(jnp.max(s_self, axis=1)))
    e_pre = jnp.exp(s_pre - top[:, None])
    e_demo = jnp.exp(s_demo - top[:, None])
    e_self = jnp.exp(s_self - top[:, None])
    total = lax.optimization_barrier(jnp.sum(e_pre, axis=1)) + lax.optimization_barrier(jnp.sum(e_demo, axis=1)) + lax.optimization_barrier(jnp.sum(e_self, axis=1))
    acc = jnp.dot((e_pre * v_scale[None, :]).astype(jnp.bfloat16), p_vals, preferred_element_type=jnp.float32)
    acc = acc + jnp.dot(e_demo.astype(jnp.bfloat16), d_vals, preferred_element_type=jnp.float32)
    acc = acc + jnp.dot(e_self.astype(jnp.bfloat16), s_vals, preferred_element_type=jnp.float32)
    return (acc / total[:, None]).astype(jnp.bfloat16)

def reference(hidden, w_query, w_key, w_value, w_out, prefix_keys, prefix_values, key_scales, value_scales, demo_keys, demo_values, task_ids, demo_lengths, offsets):
    group = HEADS // KVH
    query = jnp.dot(hidden, w_query, preferred_element_type=jnp.float32).astype(jnp.bfloat16)
    s_keys = jnp.dot(hidden, w_key, preferred_element_type=jnp.float32).astype(jnp.bfloat16)
    s_vals = jnp.dot(hidden, w_value, preferred_element_type=jnp.float32).astype(jnp.bfloat16)
    q_heads = query.reshape(QTOK, KVH, group, HD).transpose(1, 0, 2, 3).reshape(KVH, QTOK * group, HD)
    p_keys = prefix_keys.reshape(PREFIX, KVH, HD).transpose(1, 0, 2)
    p_vals = prefix_values.reshape(PREFIX, KVH, HD).transpose(1, 0, 2)
    k_scale = jnp.repeat(key_scales, BLK, axis=0).T
    v_scale = jnp.repeat(value_scales, BLK, axis=0).T
    d_keys = demo_keys.reshape(TASKS * DEMO, KVH, HD).transpose(1, 0, 2)
    d_vals = demo_values.reshape(TASKS * DEMO, KVH, HD).transpose(1, 0, 2)
    sk = s_keys.reshape(QTOK, KVH, HD).transpose(1, 0, 2)
    sv = s_vals.reshape(QTOK, KVH, HD).transpose(1, 0, 2)
    demo_task = jnp.repeat(jnp.arange(TASKS, dtype=jnp.int32), DEMO)
    demo_pos = jnp.tile(jnp.arange(DEMO, dtype=jnp.int32), TASKS)
    live = demo_pos < demo_lengths[demo_task]
    d_mask = (task_ids[:, None] == demo_task[None, :]) & live[None, :]
    s_mask = (task_ids[:, None] == task_ids[None, :]) & (offsets[None, :] <= offsets[:, None])
    d_mask = jnp.repeat(d_mask, group, axis=0)
    s_mask = jnp.repeat(s_mask, group, axis=0)

    def run(h):
        return one_head((q_heads[h], p_keys[h], p_vals[h], k_scale[h], v_scale[h], d_keys[h], d_vals[h], sk[h], sv[h], d_mask, s_mask))
    heads_out = lax.map(run, jnp.arange(KVH, dtype=jnp.int32))
    attended = heads_out.reshape(KVH, QTOK, group, HD).transpose(1, 0, 2, 3).reshape(QTOK, HEADS * HD)
    return jnp.dot(attended, w_out, preferred_element_type=jnp.float32).astype(jnp.bfloat16)
```

```python
import functools
import math

import jax
import jax.numpy as jnp
from jax import lax
from jax.experimental import pallas as pl
from jax.experimental.pallas import tpu as pltpu
from jax.sharding import PartitionSpec as P

HD = 128
NEG = -1e30
STAT = 8
F32 = jnp.float32
BF16 = jnp.bfloat16


def remote(src, dst, send, recv, dev):
    return pltpu.make_async_remote_copy(
        src_ref=src,
        dst_ref=dst,
        send_sem=send,
        recv_sem=recv,
        device_id={"seq": dev},
        device_id_type=pl.DeviceIdType.MESH,
    )


def enter(chips, chip, core):
    barrier = pltpu.get_barrier_semaphore()

    def greet(k, _):
        pl.semaphore_signal(
            barrier,
            inc=1,
            device_id={"seq": lax.rem(chip + k, chips) * 2 + core},
            device_id_type=pl.DeviceIdType.MESH,
        )
        return 0

    lax.fori_loop(1, chips, greet, 0)
    pl.semaphore_signal(
        barrier,
        inc=1,
        device_id={"seq": chip * 2 + 1 - core},
        device_id_type=pl.DeviceIdType.MESH,
    )
    pl.semaphore_wait(barrier, chips)


def gather(chips, chip, core, gat, g_send, g_recv, f_send, f_recv):
    partner = chip * 2 + 1 - core

    def to_chip(k):
        dev = lax.rem(chip + k, chips) * 2 + core
        mine = gat.at[core, chip]
        return remote(mine, gat.at[core, chip], g_send.at[k], g_recv.at[k], dev)

    def to_partner(k):
        src = lax.rem(chip - k + chips, chips)
        return remote(
            gat.at[core, src], gat.at[core, src], f_send.at[k], f_recv.at[k], partner
        )

    def from_chip(k):
        src = lax.rem(chip - k + chips, chips)
        return remote(gat.at[core, src], gat.at[core, src], g_send.at[k], g_recv.at[k], partner)

    def from_partner(k):
        src = lax.rem(chip - k + chips, chips)
        return remote(
            gat.at[1 - core, src], gat.at[1 - core, src], f_send.at[k], f_recv.at[k], partner
        )

    def start(k, _):
        to_chip(k).start()
        return 0

    lax.fori_loop(1, chips, start, 0)
    to_partner(0).start()

    def forward(k, _):
        from_chip(k).wait_recv()
        to_partner(k).start()
        return 0

    lax.fori_loop(1, chips, forward, 0)

    def arrive(k, _):
        from_partner(k).wait_recv()
        to_partner(k).wait_send()
        return 0

    lax.fori_loop(0, chips, arrive, 0)

    def drain(k, _):
        to_chip(k).wait_send()
        return 0

    lax.fori_loop(1, chips, drain, 0)


def project_kernel(
    chips, qh, kvs, hid, wq, wk, wv, out,
    wbuf, kvp, part, recv1, sums, recv2, gat,
    w_sem, s1, r1, s2, r2, g_send, g_recv, f_send, f_recv,
):
    index = lax.axis_index("seq")
    chip, core = index // 2, lax.rem(index, 2)
    partner = chip * 2 + 1 - core
    wide = qh * HD
    qt = hid.shape[0] // 2
    kvg = 2 * wk.shape[1] // HD

    def piece_of(k):
        return lax.rem(chip + 1 + k, chips)

    def load(k):
        return pltpu.make_async_copy(
            wq.at[:, pl.ds(pl.multiple_of(piece_of(k) * wide, HD), wide)],
            wbuf.at[k],
            w_sem.at[k],
        )

    def pair(k):
        return remote(part.at[1 - core, k], recv1.at[k], s1.at[k], r1.at[k], partner)

    def scatter(k):
        return remote(
            sums.at[k], recv2.at[k], s2.at[k], r2.at[k], piece_of(k) * 2 + core
        )

    def begin(k, _):
        load(k).start()
        return 0

    lax.fori_loop(0, chips, begin, 0)
    for i, w in enumerate((wk, wv)):
        res = jnp.dot(hid[...], w[...], preferred_element_type=F32)
        for g in range(kvg // 2):
            for c in range(2):
                kvp[i * (kvg // 2) + g, c] = res[c * qt : (c + 1) * qt, g * HD : (g + 1) * HD]
    enter(chips, chip, core)

    def merge(k):
        pair(k).wait_recv()
        sums[k] = part[core, k] + recv1[k]

    def step(k, _):
        load(k).wait()
        res = jnp.dot(hid[...], wbuf[k], preferred_element_type=F32)
        for c in range(2):
            for s in range(qh):
                part[c, k, s] = res[c * qt : (c + 1) * qt, s * HD : (s + 1) * HD]
            for s in range(kvs):
                part[c, k, qh + s] = kvp[lax.rem(piece_of(k) * kvs + s, kvg), c]
        pair(k).start()

        @pl.when(k > 0)
        def _():
            merge(k - 1)
            scatter(k - 1).start()

        return 0

    lax.fori_loop(0, chips, step, 0)
    merge(chips - 1)

    def collect(k, total):
        scatter(k).wait_recv()
        return total + recv2[k]

    total = lax.fori_loop(0, chips - 1, collect, sums[chips - 1])
    gat[core, chip] = total.astype(BF16)
    gather(chips, chip, core, gat, g_send, g_recv, f_send, f_recv)

    def drain(k, _):
        pair(k).wait_send()
        return 0

    lax.fori_loop(0, chips, drain, 0)

    def drain2(k, _):
        scatter(k).wait_send()
        return 0

    lax.fori_loop(0, chips - 1, drain2, 0)
    out[...] = gat[...]


def nt(a, b):
    return lax.dot_general(a, b, (((1,), (1,)), ((), ())), preferred_element_type=F32)


def tn(a, b):
    return lax.dot_general(a, b, (((0,), (0,)), ((), ())), preferred_element_type=F32)


def attend_kernel(
    qh, blk, ks, vs, q_ref, sk, sv, pk, pv, dk, dv, task_row, len_row, s_mask, out,
    s_scr, acc,
):
    h = pl.program_id(0)
    inv = 1.0 / math.sqrt(HD)
    per_head = q_ref.shape[1]
    qt = q_ref.shape[3]
    cols = qh * qt
    rows = 2 * per_head * cols
    q = jnp.concatenate(
        [q_ref[c, p, :qh].reshape(cols, HD) for c in range(2) for p in range(per_head)], axis=0
    )
    blocks = pk.shape[0] // blk
    many = math.gcd(4, blocks)
    tasks, demo_dev = dk.shape[0], dk.shape[1]
    some = math.gcd(4, tasks)

    def fold(x, op):
        return op(x.reshape(x.shape[0] // 8, 8, x.shape[1]), axis=0)

    def score(i, top):
        for b in range(many):
            at = i * many + b
            here = pl.ds(pl.multiple_of(at * blk, blk), blk)
            s = nt(pk[here, :], q) * (ks[at, h] * inv)
            s_scr[here, :] = s
            top = jnp.maximum(top, fold(s, jnp.max))
        return top

    top = lax.fori_loop(0, blocks // many, score, jnp.full((8, rows), NEG, F32))
    mine = task_row[...]

    def pick(i, best):
        for b in range(some):
            best = jnp.where(mine == i * some + b, nt(dk[i * some + b], q), best)
        return best

    s_demo = lax.fori_loop(0, tasks // some, pick, jnp.zeros((demo_dev, rows), F32))
    slot = lax.broadcasted_iota(jnp.int32, (demo_dev, rows), 0)
    s_demo = jnp.where(slot < len_row[...], s_demo * inv, NEG)
    self_k = jnp.concatenate([sk[c, 0, 0] for c in range(2)], axis=0)
    self_v = jnp.concatenate([sv[c, 0, 0] for c in range(2)], axis=0)
    s_self = jnp.where(s_mask[...] > 0, nt(self_k, q) * inv, NEG)
    top = jnp.maximum(top, jnp.maximum(fold(s_demo, jnp.max), fold(s_self, jnp.max)))
    top = jnp.max(top, axis=0, keepdims=True)

    e_demo = jnp.exp(s_demo - top)
    e_self = jnp.exp(s_self - top)
    total = fold(e_demo, jnp.sum) + fold(e_self, jnp.sum)
    acc[...] = tn(self_v, e_self.astype(BF16))

    def demo(i, _):
        weights = jnp.concatenate(
            [jnp.where(mine == i * some + b, e_demo, 0.0).astype(BF16) for b in range(some)], axis=0
        )
        here = pl.ds(i * some, some)
        acc[...] += tn(dv[here].reshape(some * demo_dev, HD), weights)
        return 0

    lax.fori_loop(0, tasks // some, demo, 0)

    def prefix(i, total):
        weights = []
        for b in range(many):
            at = i * many + b
            e = jnp.exp(s_scr[pl.ds(pl.multiple_of(at * blk, blk), blk), :] - top)
            total = total + fold(e, jnp.sum)
            weights.append((e * vs[at, h]).astype(BF16))
        here = pl.ds(pl.multiple_of(i * many * blk, blk), many * blk)
        acc[...] += tn(pv[here, :], jnp.concatenate(weights, axis=0))
        return total

    total = lax.fori_loop(0, blocks // many, prefix, total)
    total = jnp.sum(total, axis=0, keepdims=True)
    first = lax.broadcasted_iota(jnp.int32, (STAT, rows), 0) == 0
    stats = jnp.where(first, top, total)
    for c in range(2):
        for p in range(per_head):
            lanes = slice((c * per_head + p) * cols, (c * per_head + p + 1) * cols)
            out[c, p, :HD] = acc[:, lanes]
            out[c, p, HD:] = stats[:, lanes]


def output_kernel(
    chips, qh, part, wo, out,
    wbuf, recv1, sums, recv2, gat, acc,
    w_sem, s1, r1, s2, r2, g_send, g_recv, f_send, f_recv,
):
    index = lax.axis_index("seq")
    chip, core = index // 2, lax.rem(index, 2)
    partner = chip * 2 + 1 - core
    deep = qh * HD
    cols = part.shape[3]
    qt = cols // qh

    def piece_of(k):
        return lax.rem(chip + 1 + k, chips)

    def load(k):
        return pltpu.make_async_copy(
            wo.at[pl.ds(pl.multiple_of(k * deep, HD), deep), :], wbuf.at[k], w_sem.at[k]
        )

    def pair(k):
        return remote(part.at[1 - core, piece_of(k)], recv1.at[k], s1.at[k], r1.at[k], partner)

    def scatter(k):
        return remote(
            sums.at[k], recv2.at[k], s2.at[k], r2.at[k], piece_of(k) * 2 + core
        )

    enter(chips, chip, core)

    def begin(k, _):
        pair(k).start()
        return 0

    lax.fori_loop(0, chips, begin, 0)

    def begin_load(k, _):
        load(k).start()
        return 0

    lax.fori_loop(0, chips, begin_load, 0)

    def join(a, b):
        top = jnp.maximum(a[HD : HD + 1], b[HD : HD + 1])
        fa, fb = jnp.exp(a[HD : HD + 1] - top), jnp.exp(b[HD : HD + 1] - top)
        first = lax.broadcasted_iota(jnp.int32, (STAT, cols), 0) == 0
        stats = jnp.where(first, top, a[HD:] * fa + b[HD:] * fb)
        return a[:HD] * fa + b[:HD] * fb, stats

    def merge(k):
        pair(k).wait_recv()
        low, stats = join(part[core, piece_of(k)], recv1[k])
        sums[k, :HD] = low
        sums[k, HD:] = stats

    def step(k, _):
        merge(k)
        scatter(k).start()
        return 0

    lax.fori_loop(0, chips - 1, step, 0)
    merge(chips - 1)

    def arrive(k, _):
        scatter(k).wait_recv()
        return 0

    lax.fori_loop(0, chips - 1, arrive, 0)
    own = chips - 1
    top = sums[own, HD : HD + 1]
    for k in range(own):
        top = jnp.maximum(top, recv2[k, HD : HD + 1])
    factor = jnp.exp(sums[own, HD : HD + 1] - top)
    total = sums[own, HD + 1 : HD + 2] * factor
    value = sums[own, :HD] * factor
    for k in range(own):
        factor = jnp.exp(recv2[k, HD : HD + 1] - top)
        total = total + recv2[k, HD + 1 : HD + 2] * factor
        value = value + recv2[k, :HD] * factor
    rows = (value / total).T.astype(BF16)
    gat[core, chip] = rows.reshape(qh, qt, HD)
    gather(chips, chip, core, gat, g_send, g_recv, f_send, f_recv)

    def drain(k, _):
        pair(k).wait_send()
        return 0

    lax.fori_loop(0, chips, drain, 0)

    def drain2(k, _):
        scatter(k).wait_send()
        return 0

    lax.fori_loop(0, chips - 1, drain2, 0)
    acc[...] = jnp.zeros_like(acc)

    def mix(k, _):
        load(k).wait()
        left = jnp.concatenate(
            [jnp.concatenate([gat[c, k, s] for s in range(qh)], axis=1) for c in range(2)], axis=0
        )
        acc[...] += jnp.dot(left, wbuf[k], preferred_element_type=F32)
        return 0

    lax.fori_loop(0, chips, mix, 0)
    out[...] = acc[...].astype(BF16)


def sems(chips):
    return [pltpu.SemaphoreType.DMA((chips,)) for _ in range(9)]


def body(
    hidden, w_query, w_key, w_value, w_out, prefix_keys, prefix_values, key_scales, value_scales,
    demo_keys, demo_values, task_ids, demo_lengths, offsets,
):
    devices = lax.axis_size("seq")
    index = lax.axis_index("seq")
    chips = devices // 2
    qtok, depth = hidden.shape
    qt = qtok // 2
    kvh = prefix_keys.shape[1] // HD
    heads = w_query.shape[1] // HD
    group = heads // kvh
    qh = heads // chips
    kvs = max(1, 2 * kvh // chips)
    gp = qh + kvs
    cols = qh * qt
    per_head = chips // kvh
    tasks, demo_dev = demo_keys.shape[:2]
    pre_dev = prefix_keys.shape[0]
    blk = pre_dev // key_scales.shape[0]
    rows = qtok * group
    vmem = pl.BlockSpec(memory_space=pltpu.VMEM)
    hbm = pl.BlockSpec(memory_space=pl.ANY)

    query = pl.pallas_call(
        functools.partial(project_kernel, chips, qh, kvs),
        name="project",
        out_shape=jax.ShapeDtypeStruct((2, chips, gp, qt, HD), BF16),
        in_specs=[vmem, hbm, vmem, vmem],
        out_specs=vmem,
        scratch_shapes=[
            pltpu.VMEM((chips, depth, qh * HD), BF16),
            pltpu.VMEM((2 * kvh, 2, qt, HD), F32),
            pltpu.VMEM((2, chips, gp, qt, HD), F32),
            pltpu.VMEM((chips, gp, qt, HD), F32),
            pltpu.VMEM((chips, gp, qt, HD), F32),
            pltpu.VMEM((chips, gp, qt, HD), F32),
            pltpu.VMEM((2, chips, gp, qt, HD), BF16),
        ]
        + sems(chips),
        compiler_params=pltpu.CompilerParams(
            collective_id=0, has_side_effects=True, vmem_limit_bytes=48 << 20
        ),
    )(hidden, w_query, w_key, w_value)

    def by_row(x):
        return jnp.broadcast_to(x.reshape(2, 1, qt), (2, group, qt)).reshape(1, rows)

    task_row = by_row(task_ids)
    task_len = jnp.sum(
        jnp.where(task_ids[:, None] == jnp.arange(tasks)[None, :], demo_lengths[None, :], 0), axis=1
    )
    len_row = by_row(task_len - index * demo_dev)
    token = jnp.arange(qtok, dtype=jnp.int32)
    s_mask = (
        (task_ids[:, None] == task_row)
        & (offsets[:, None] <= by_row(offsets))
        & (lax.rem(token, devices) == index)[:, None]
    ).astype(jnp.int32)

    def kv_spec(first):
        return pl.BlockSpec(
            (2, 1, 1, qt, HD),
            lambda h: (0, (first + h) // kvs, qh + (first + h) % kvs, 0, 0),
        )

    def whole(shape):
        return pl.BlockSpec(shape, lambda h: (0, 0))

    smem = pl.BlockSpec(memory_space=pltpu.SMEM)
    pre_spec = pl.BlockSpec((pre_dev, HD), lambda h: (0, h))
    demo_spec = pl.BlockSpec((tasks, demo_dev, HD), lambda h: (0, 0, h))
    part = pl.pallas_call(
        functools.partial(attend_kernel, qh, blk),
        name="attend",
        grid=(kvh,),
        out_shape=jax.ShapeDtypeStruct((2, chips, HD + STAT, cols), F32),
        in_specs=[
            smem,
            smem,
            pl.BlockSpec((2, per_head, gp, qt, HD), lambda h: (0, h, 0, 0, 0)),
            kv_spec(0),
            kv_spec(kvh),
            pre_spec,
            pre_spec,
            demo_spec,
            demo_spec,
            whole((1, rows)),
            whole((1, rows)),
            whole((qtok, rows)),
        ],
        out_specs=pl.BlockSpec((2, per_head, HD + STAT, cols), lambda h: (0, h, 0, 0)),
        scratch_shapes=[pltpu.VMEM((pre_dev, rows), F32), pltpu.VMEM((HD, rows), F32)],
        compiler_params=pltpu.CompilerParams(vmem_limit_bytes=40 << 20),
    )(
        key_scales, value_scales, query, query, query, prefix_keys, prefix_values,
        demo_keys, demo_values, task_row, len_row, s_mask,
    )

    return pl.pallas_call(
        functools.partial(output_kernel, chips, qh),
        name="mix",
        out_shape=jax.ShapeDtypeStruct((qtok, w_out.shape[1]), BF16),
        in_specs=[vmem, hbm],
        out_specs=vmem,
        scratch_shapes=[
            pltpu.VMEM((chips, qh * HD, w_out.shape[1]), BF16),
            pltpu.VMEM((chips, HD + STAT, cols), F32),
            pltpu.VMEM((chips, HD + STAT, cols), F32),
            pltpu.VMEM((chips, HD + STAT, cols), F32),
            pltpu.VMEM((2, chips, qh, qt, HD), BF16),
            pltpu.VMEM((qtok, w_out.shape[1]), F32),
        ]
        + sems(chips),
        compiler_params=pltpu.CompilerParams(
            collective_id=1, has_side_effects=True, vmem_limit_bytes=48 << 20
        ),
    )(part, w_out)


def solution(mesh):
    placed = (
        P("groups", "seq"),
        P("seq", None),
        P("seq", None),
        P("seq", None),
        P(None, "seq"),
        P(("groups", "seq"), None),
        P(("groups", "seq"), None),
        P(("groups", "seq"), None),
        P(("groups", "seq"), None),
        P("groups", "seq", None),
        P("groups", "seq", None),
        P("groups"),
        P("groups"),
        P("groups"),
    )
    return jax.shard_map(
        body, mesh=mesh, in_specs=placed, out_specs=P("groups", "seq"), check_vma=False
    )
```

```python
import functools
import math

import jax
import jax.numpy as jnp
from jax import lax
from jax.experimental import pallas as pl
from jax.experimental.pallas import tpu as pltpu
from jax.sharding import PartitionSpec as P

HD = 128
NEG = -1e30
STAT = 8
F32 = jnp.float32
BF16 = jnp.bfloat16


def remote(src, dst, send, recv, dev):
    return pltpu.make_async_remote_copy(
        src_ref=src,
        dst_ref=dst,
        send_sem=send,
        recv_sem=recv,
        device_id={"seq": dev},
        device_id_type=pl.DeviceIdType.MESH,
    )


def spot(chips, k):
    index = lax.axis_index("seq")
    chip, core = index // 2, lax.rem(index, 2)
    far, near = chip // 2, lax.rem(chip, 2)
    side = lax.rem(1 - near + lax.rem(k, 2), 2)
    return lax.rem(far + 1 + k // 2, chips // 2) * 2 + side


def enter(chips, chip, core):
    barrier = pltpu.get_barrier_semaphore()
    far, near = chip // 2, lax.rem(chip, 2)

    def hello(dev):
        pl.semaphore_signal(
            barrier, inc=1, device_id={"seq": dev}, device_id_type=pl.DeviceIdType.MESH
        )

    def greet(k, _):
        hello((lax.rem(far + k, chips // 2) * 2 + near) * 2 + core)
        return 0

    lax.fori_loop(1, chips // 2, greet, 0)
    hello((far * 2 + 1 - near) * 2 + core)
    hello(chip * 2 + 1 - core)
    pl.semaphore_wait(barrier, chips // 2 + 1)


def gather(chips, chip, core, gat, sem, use):
    z_send, z_recv, y_send, y_recv, f_send, f_recv = sem
    depth = chips // 2
    far, near = chip // 2, lax.rem(chip, 2)

    def from_far(i, side):
        return lax.rem(far - i + depth, depth) * 2 + side

    def move(c, piece, send, recv, dev):
        return remote(gat.at[c, piece], gat.at[c, piece], send, recv, dev)

    def to_far(i):
        dev = (lax.rem(far + i, depth) * 2 + near) * 2 + core
        return move(core, chip, z_send.at[i], z_recv.at[i], dev)

    def of_far(i):
        dev = (lax.rem(far + i, depth) * 2 + near) * 2 + core
        return move(core, from_far(i, near), z_send.at[i], z_recv.at[i], dev)

    def near_copy(i, side):
        dev = (far * 2 + 1 - near) * 2 + core
        return move(core, from_far(i, side), y_send.at[i], y_recv.at[i], dev)

    def core_copy(c, i, e):
        side = near if e == 0 else 1 - near
        k = 2 * i + e
        return move(c, from_far(i, side), f_send.at[k], f_recv.at[k], chip * 2 + 1 - core)

    def start(i, _):
        to_far(i).start()
        return 0

    lax.fori_loop(1, depth, start, 0)
    near_copy(0, near).start()
    core_copy(core, 0, 0).start()

    def forward(i, _):
        of_far(i).wait_recv()
        near_copy(i, near).start()
        core_copy(core, i, 0).start()
        near_copy(i - 1, 1 - near).wait_recv()
        core_copy(core, i - 1, 1).start()
        return 0

    lax.fori_loop(1, depth, forward, 0)
    near_copy(depth - 1, 1 - near).wait_recv()
    core_copy(core, depth - 1, 1).start()

    def arrive(i, _):
        for e in range(2):
            core_copy(1 - core, i, e).wait_recv()
            use(from_far(i, near if e == 0 else 1 - near))
        return 0

    lax.fori_loop(0, depth, arrive, 0)

    def drain(i, _):
        near_copy(i, near).wait_send()
        core_copy(core, i, 0).wait_send()
        core_copy(core, i, 1).wait_send()

        @pl.when(i > 0)
        def _():
            to_far(i).wait_send()

        return 0

    lax.fori_loop(0, depth, drain, 0)


def project_kernel(
    chips, qh, kvs, hid_hbm, wq, wk_hbm, wv_hbm, out,
    hid, wk, wv, wbuf, kvp, part, recv1, sums, recv_y, far_sum, recv_z, gat,
    in_sem, w_sem, s1, r1, sy, ry, sz, rz, *g_sem,
):
    index = lax.axis_index("seq")
    chip, core = index // 2, lax.rem(index, 2)
    depth = chips // 2
    far, near = chip // 2, lax.rem(chip, 2)
    wide = qh * HD
    qt = hid.shape[0] // 2
    kvg = 2 * wk.shape[1] // HD

    def load(k):
        return pltpu.make_async_copy(
            wq.at[:, pl.ds(pl.multiple_of(spot(chips, k) * wide, HD), wide)],
            wbuf.at[k],
            w_sem.at[k],
        )

    def pair(k):
        dev = chip * 2 + 1 - core
        return remote(part.at[1 - core, k], recv1.at[k], s1.at[k], r1.at[k], dev)

    def near_send(i):
        dev = (far * 2 + 1 - near) * 2 + core
        return remote(sums.at[2 * i], recv_y.at[i], sy.at[i], ry.at[i], dev)

    def far_send(i):
        dev = (lax.rem(far + 1 + i, depth) * 2 + near) * 2 + core
        return remote(far_sum.at[i], recv_z.at[i], sz.at[i], rz.at[i], dev)

    small = [
        pltpu.make_async_copy(src, dst, in_sem.at[i])
        for i, (src, dst) in enumerate(((hid_hbm, hid), (wk_hbm, wk), (wv_hbm, wv)))
    ]
    for copy in small:
        copy.start()

    def begin(k, _):
        load(k).start()
        return 0

    lax.fori_loop(0, chips, begin, 0)
    enter(chips, chip, core)
    for copy in small:
        copy.wait()
    for i, w in enumerate((wk, wv)):
        res = jnp.dot(hid[...], w[...], preferred_element_type=F32)
        for g in range(kvg // 2):
            for c in range(2):
                kvp[i * (kvg // 2) + g, c] = res[c * qt : (c + 1) * qt, g * HD : (g + 1) * HD]

    def step(i, _):
        @pl.when(i < depth)
        def _():
            for e in range(2):
                k = 2 * i + e
                load(k).wait()
                res = jnp.dot(hid[...], wbuf[k], preferred_element_type=F32)
                for c in range(2):
                    for s in range(qh):
                        part[c, k, s] = res[c * qt : (c + 1) * qt, s * HD : (s + 1) * HD]
                    for s in range(kvs):
                        part[c, k, qh + s] = kvp[lax.rem(spot(chips, k) * kvs + s, kvg), c]
                pair(k).start()

        @pl.when((i > 0) & (i <= depth))
        def _():
            for e in range(2):
                k = 2 * (i - 1) + e
                pair(k).wait_recv()
                sums[k] = part[core, k] + recv1[k]
                if e == 0:
                    near_send(i - 1).start()

        @pl.when(i > 1)
        def _():
            j = i - 2
            near_send(j).wait_recv()
            far_sum[j] = sums[2 * j + 1] + recv_y[j]

            @pl.when(j < depth - 1)
            def _():
                far_send(j).start()

        return 0

    lax.fori_loop(0, depth + 2, step, 0)

    def collect(i, total):
        far_send(i).wait_recv()
        return total + recv_z[i]

    total = lax.fori_loop(0, depth - 1, collect, far_sum[depth - 1])
    gat[core, chip] = total.astype(BF16)
    gather(chips, chip, core, gat, g_sem, lambda piece: None)

    def drain(i, _):
        pair(2 * i).wait_send()
        pair(2 * i + 1).wait_send()
        near_send(i).wait_send()

        @pl.when(i < depth - 1)
        def _():
            far_send(i).wait_send()

        return 0

    lax.fori_loop(0, depth, drain, 0)
    out[...] = gat[...]


def nt(a, b):
    return lax.dot_general(a, b, (((1,), (1,)), ((), ())), preferred_element_type=F32)


def tn(a, b):
    return lax.dot_general(a, b, (((0,), (0,)), ((), ())), preferred_element_type=F32)


def attend_kernel(
    devices, qh, blk, ks, vs, tasks_of, lens, offs, q_ref, sk, sv, pk, pv, dk, dv, out,
    s_scr, acc, task_row, len_row, s_mask,
):
    h = pl.program_id(0)
    inv = 1.0 / math.sqrt(HD)
    per_head = q_ref.shape[1]
    qt = q_ref.shape[3]
    cols = qh * qt
    rows = 2 * per_head * cols
    q = jnp.concatenate(
        [q_ref[c, p, :qh].reshape(cols, HD) for c in range(2) for p in range(per_head)], axis=0
    )
    blocks = pk.shape[0] // blk
    many = math.gcd(4, blocks)
    tasks, demo_dev = dk.shape[0], dk.shape[1]
    some = math.gcd(4, tasks)

    @pl.when(h == 0)
    def _():
        index = lax.axis_index("seq")
        lane = lax.broadcasted_iota(jnp.int32, (1, rows), 1)
        token = (lane // (rows // 2)) * qt + lax.rem(lane, qt)
        zero = jnp.zeros((1, rows), jnp.int32)

        def spread(t, carry):
            task = tasks_of[t]
            here = token == t
            left = lens[task] - index * demo_dev
            values = (task, left, offs[t])
            return tuple(jnp.where(here, v, old) for v, old in zip(values, carry))

        task_all, len_all, off_all = lax.fori_loop(0, 2 * qt, spread, (zero, zero, zero))
        task_row[...] = task_all
        len_row[...] = len_all

        def allow(u, _):
            mine = jnp.where(lax.rem(u, devices) == index, tasks_of[u], -1)
            keep = (task_all == mine) & (off_all >= offs[u])
            s_mask[pl.ds(u, 1), :] = keep.astype(jnp.int32)
            return 0

        lax.fori_loop(0, 2 * qt, allow, 0)

    def fold(x, op):
        return op(x.reshape(x.shape[0] // 8, 8, x.shape[1]), axis=0)

    def score(i, top):
        for b in range(many):
            at = i * many + b
            here = pl.ds(pl.multiple_of(at * blk, blk), blk)
            s = nt(pk[here, :], q) * (ks[h, at] * inv)
            s_scr[here, :] = s
            top = jnp.maximum(top, fold(s, jnp.max))
        return top

    top = lax.fori_loop(0, blocks // many, score, jnp.full((8, rows), NEG, F32))
    mine = task_row[...]

    def pick(i, best):
        for b in range(some):
            best = jnp.where(mine == i * some + b, nt(dk[i * some + b], q), best)
        return best

    s_demo = lax.fori_loop(0, tasks // some, pick, jnp.zeros((demo_dev, rows), F32))
    slot = lax.broadcasted_iota(jnp.int32, (demo_dev, rows), 0)
    s_demo = jnp.where(slot < len_row[...], s_demo * inv, NEG)
    self_k = jnp.concatenate([sk[c, 0, 0] for c in range(2)], axis=0)
    self_v = jnp.concatenate([sv[c, 0, 0] for c in range(2)], axis=0)
    s_self = jnp.where(s_mask[...] > 0, nt(self_k, q) * inv, NEG)
    top = jnp.maximum(top, jnp.maximum(fold(s_demo, jnp.max), fold(s_self, jnp.max)))
    top = jnp.max(top, axis=0, keepdims=True)

    e_demo = jnp.exp(s_demo - top)
    e_self = jnp.exp(s_self - top)
    total = fold(e_demo, jnp.sum) + fold(e_self, jnp.sum)
    acc[...] = tn(self_v, e_self.astype(BF16))

    def demo(i, _):
        weights = jnp.concatenate(
            [jnp.where(mine == i * some + b, e_demo, 0.0).astype(BF16) for b in range(some)], axis=0
        )
        here = pl.ds(i * some, some)
        acc[...] += tn(dv[here].reshape(some * demo_dev, HD), weights)
        return 0

    lax.fori_loop(0, tasks // some, demo, 0)

    def prefix(i, total):
        weights = []
        for b in range(many):
            at = i * many + b
            e = jnp.exp(s_scr[pl.ds(pl.multiple_of(at * blk, blk), blk), :] - top)
            total = total + fold(e, jnp.sum)
            weights.append((e * vs[h, at]).astype(BF16))
        here = pl.ds(pl.multiple_of(i * many * blk, blk), many * blk)
        acc[...] += tn(pv[here, :], jnp.concatenate(weights, axis=0))
        return total

    total = lax.fori_loop(0, blocks // many, prefix, total)
    total = jnp.sum(total, axis=0, keepdims=True)
    first = lax.broadcasted_iota(jnp.int32, (STAT, rows), 0) == 0
    stats = jnp.where(first, top, total)
    for c in range(2):
        for p in range(per_head):
            lanes = slice((c * per_head + p) * cols, (c * per_head + p + 1) * cols)
            out[c, p, :HD] = acc[:, lanes]
            out[c, p, HD:] = stats[:, lanes]


def output_kernel(
    chips, qh, part, wo, out,
    wbuf, recv1, keep, y_val, y_stat, yr_val, yr_stat, z_val, z_stat, zr_val, zr_stat, gat, acc,
    w_sem, s1, r1, sy, ry, sz, rz, sy2, ry2, sz2, rz2, *g_sem,
):
    index = lax.axis_index("seq")
    chip, core = index // 2, lax.rem(index, 2)
    depth = chips // 2
    far, near = chip // 2, lax.rem(chip, 2)
    deep = qh * HD
    cols = part.shape[3]
    qt = cols // qh

    def load(k):
        return pltpu.make_async_copy(
            wo.at[pl.ds(pl.multiple_of(k * deep, HD), deep), :], wbuf.at[k], w_sem.at[k]
        )

    def pair(k):
        dev = chip * 2 + 1 - core
        src = part.at[1 - core, spot(chips, k)]
        return remote(src, recv1.at[k], s1.at[k], r1.at[k], dev)

    def near_send(i):
        dev = (far * 2 + 1 - near) * 2 + core
        return (
            remote(y_stat.at[i], yr_stat.at[i], sy2.at[i], ry2.at[i], dev),
            remote(y_val.at[i], yr_val.at[i], sy.at[i], ry.at[i], dev),
        )

    def far_send(i):
        dev = (lax.rem(far + 1 + i, depth) * 2 + near) * 2 + core
        return (
            remote(z_stat.at[i], zr_stat.at[i], sz2.at[i], rz2.at[i], dev),
            remote(z_val.at[i], zr_val.at[i], sz.at[i], rz.at[i], dev),
        )

    enter(chips, chip, core)

    def begin(k, _):
        pair(k).start()
        return 0

    lax.fori_loop(0, chips, begin, 0)

    def begin_load(k, _):
        load(k).start()
        return 0

    lax.fori_loop(0, chips, begin_load, 0)
    first = lax.broadcasted_iota(jnp.int32, (STAT, cols), 0) == 0

    def join(a, a_stat, b, b_stat):
        top = jnp.maximum(a_stat[:1], b_stat[:1])
        fa, fb = jnp.exp(a_stat[:1] - top), jnp.exp(b_stat[:1] - top)
        stat = jnp.where(first, top, a_stat * fa + b_stat * fb)
        return a.astype(F32) * fa + b.astype(F32) * fb, stat

    def merge(k):
        pair(k).wait_recv()
        at = spot(chips, k)
        return join(part[core, at, :HD], part[core, at, HD:], recv1[k, :HD], recv1[k, HD:])

    def step(i, _):
        @pl.when(i < depth)
        def _():
            value, stat = merge(2 * i)
            y_val[i] = value.astype(BF16)
            y_stat[i] = stat
            for copy in near_send(i):
                copy.start()
            value, stat = merge(2 * i + 1)
            keep[i, :HD] = value
            keep[i, HD:] = stat

        @pl.when(i > 0)
        def _():
            j = i - 1
            for copy in near_send(j):
                copy.wait_recv()
            value, stat = join(keep[j, :HD], keep[j, HD:], yr_val[j], yr_stat[j])

            @pl.when(j < depth - 1)
            def _():
                z_val[j] = value.astype(BF16)
                z_stat[j] = stat
                for copy in far_send(j):
                    copy.start()

            @pl.when(j == depth - 1)
            def _():
                keep[j, :HD] = value
                keep[j, HD:] = stat

        return 0

    lax.fori_loop(0, depth + 1, step, 0)

    def arrive(i, _):
        for copy in far_send(i):
            copy.wait_recv()
        return 0

    lax.fori_loop(0, depth - 1, arrive, 0)
    own = depth - 1
    top = keep[own, HD : HD + 1]
    for k in range(own):
        top = jnp.maximum(top, zr_stat[k, :1])
    factor = jnp.exp(keep[own, HD : HD + 1] - top)
    total = keep[own, HD + 1 : HD + 2] * factor
    value = keep[own, :HD] * factor
    for k in range(own):
        factor = jnp.exp(zr_stat[k, :1] - top)
        total = total + zr_stat[k, 1:2] * factor
        value = value + zr_val[k].astype(F32) * factor
    rows = (value / total).T.astype(BF16)
    gat[core, chip] = rows.reshape(qh, qt, HD)
    acc[...] = jnp.zeros_like(acc)

    def mix(piece):
        load(piece).wait()
        left = jnp.concatenate(
            [
                jnp.concatenate([gat[c, piece, s] for s in range(qh)], axis=1)
                for c in range(2)
            ],
            axis=0,
        )
        acc[...] += jnp.dot(left, wbuf[piece], preferred_element_type=F32)

    gather(chips, chip, core, gat, g_sem, mix)

    def drain(i, _):
        pair(2 * i).wait_send()
        pair(2 * i + 1).wait_send()
        for copy in near_send(i):
            copy.wait_send()

        @pl.when(i < depth - 1)
        def _():
            for copy in far_send(i):
                copy.wait_send()

        return 0

    lax.fori_loop(0, depth, drain, 0)
    out[...] = acc[...].astype(BF16)


def sems(*counts):
    return [pltpu.SemaphoreType.DMA((n,)) for n in counts]


def body(
    hidden, w_query, w_key, w_value, w_out, prefix_keys, prefix_values, key_scales, value_scales,
    demo_keys, demo_values, task_ids, demo_lengths, offsets,
):
    devices = lax.axis_size("seq")
    chips = devices // 2
    half = chips // 2
    qtok, depth = hidden.shape
    qt = qtok // 2
    kvh = prefix_keys.shape[1] // HD
    heads = w_query.shape[1] // HD
    group = heads // kvh
    qh = heads // chips
    kvs = max(1, 2 * kvh // chips)
    gp = qh + kvs
    cols = qh * qt
    per_head = chips // kvh
    tasks, demo_dev = demo_keys.shape[:2]
    pre_dev = prefix_keys.shape[0]
    blk = pre_dev // key_scales.shape[0]
    rows = qtok * group
    vmem = pl.BlockSpec(memory_space=pltpu.VMEM)
    hbm = pl.BlockSpec(memory_space=pltpu.HBM)

    query = pl.pallas_call(
        functools.partial(project_kernel, chips, qh, kvs),
        name="project",
        out_shape=jax.ShapeDtypeStruct((2, chips, gp, qt, HD), BF16),
        in_specs=[hbm, hbm, hbm, hbm],
        out_specs=vmem,
        scratch_shapes=[
            pltpu.VMEM(hidden.shape, BF16),
            pltpu.VMEM(w_key.shape, BF16),
            pltpu.VMEM(w_value.shape, BF16),
            pltpu.VMEM((chips, depth, qh * HD), BF16),
            pltpu.VMEM((2 * kvh, 2, qt, HD), F32),
            pltpu.VMEM((2, chips, gp, qt, HD), F32),
            pltpu.VMEM((chips, gp, qt, HD), F32),
            pltpu.VMEM((chips, gp, qt, HD), F32),
            pltpu.VMEM((half, gp, qt, HD), F32),
            pltpu.VMEM((half, gp, qt, HD), F32),
            pltpu.VMEM((half, gp, qt, HD), F32),
            pltpu.VMEM((2, chips, gp, qt, HD), BF16),
        ]
        + sems(3, chips, chips, chips, *[half] * 8, chips, chips),
        compiler_params=pltpu.CompilerParams(
            collective_id=0, has_side_effects=True, vmem_limit_bytes=48 << 20
        ),
    )(hidden, w_query, w_key, w_value)

    def kv_spec(first):
        return pl.BlockSpec(
            (2, 1, 1, qt, HD),
            lambda h: (0, (first + h) // kvs, qh + (first + h) % kvs, 0, 0),
        )

    smem = pl.BlockSpec(memory_space=pltpu.SMEM)
    pre_spec = pl.BlockSpec((pre_dev, HD), lambda h: (0, h))
    demo_spec = pl.BlockSpec((tasks, demo_dev, HD), lambda h: (0, 0, h))
    part = pl.pallas_call(
        functools.partial(attend_kernel, devices, qh, blk),
        name="attend",
        grid=(kvh,),
        out_shape=jax.ShapeDtypeStruct((2, chips, HD + STAT, cols), F32),
        in_specs=[
            *[smem] * 5,
            pl.BlockSpec((2, per_head, gp, qt, HD), lambda h: (0, h, 0, 0, 0)),
            kv_spec(0),
            kv_spec(kvh),
            pre_spec,
            pre_spec,
            demo_spec,
            demo_spec,
        ],
        out_specs=pl.BlockSpec((2, per_head, HD + STAT, cols), lambda h: (0, h, 0, 0)),
        scratch_shapes=[
            pltpu.VMEM((pre_dev, rows), F32),
            pltpu.VMEM((HD, rows), F32),
            pltpu.VMEM((1, rows), jnp.int32),
            pltpu.VMEM((1, rows), jnp.int32),
            pltpu.VMEM((qtok, rows), jnp.int32),
        ],
        compiler_params=pltpu.CompilerParams(vmem_limit_bytes=40 << 20),
    )(
        key_scales.T, value_scales.T, task_ids, demo_lengths, offsets, query, query, query,
        prefix_keys, prefix_values, demo_keys, demo_values,
    )

    return pl.pallas_call(
        functools.partial(output_kernel, chips, qh),
        name="mix",
        out_shape=jax.ShapeDtypeStruct((qtok, w_out.shape[1]), BF16),
        in_specs=[vmem, hbm],
        out_specs=vmem,
        scratch_shapes=[
            pltpu.VMEM((chips, qh * HD, w_out.shape[1]), BF16),
            pltpu.VMEM((chips, HD + STAT, cols), F32),
            pltpu.VMEM((half, HD + STAT, cols), F32),
            *[
                pltpu.VMEM((half, extent, cols), kind)
                for _ in range(4)
                for extent, kind in ((HD, BF16), (STAT, F32))
            ],
            pltpu.VMEM((2, chips, qh, qt, HD), BF16),
            pltpu.VMEM((qtok, w_out.shape[1]), F32),
        ]
        + sems(chips, chips, chips, *[half] * 12, chips, chips),
        compiler_params=pltpu.CompilerParams(
            collective_id=1, has_side_effects=True, vmem_limit_bytes=48 << 20
        ),
    )(part, w_out)


def solution(mesh):
    placed = (
        P("groups", "seq"),
        P("seq", None),
        P("seq", None),
        P("seq", None),
        P(None, "seq"),
        P(("groups", "seq"), None),
        P(("groups", "seq"), None),
        P(("groups", "seq"), None),
        P(("groups", "seq"), None),
        P("groups", "seq", None),
        P("groups", "seq", None),
        P("groups"),
        P("groups"),
        P("groups"),
    )
    return jax.shard_map(
        body, mesh=mesh, in_specs=placed, out_specs=P("groups", "seq"), check_vma=False
    )
```
